128 devices in a mesh: users: 128 (over y, z, x, core).
Axes of the slice: x: 4, y: 4, z: 4, core: 2. Of those that a mesh axis runs over, the one named last changes fastest.
Arguments:
- tile_owner: int32 [16384, 1], P('users'), may hold values from 0 to 127; in each aligned block of 128 rows (0 to 127, 128 to 255, ...) at most 2 rows name the same one
- tile_slot: int32 [16384], P('users'), may hold values from 0 to 15
- tile_cblock: int32 [16384], P('users'), may hold values from 0 to 63
- tile_context: int32 [16384, 512], P('users'), may hold values from 0 to 7
- tile_weights: bfloat16 [16384, 128, 512], P('users'), as said below
- item_factors: bfloat16 [2048, 64, 128], P('users'), may hold values from -0.5 to 0.5
- context_factors: bfloat16 [8, 512], replicated, may hold values from -0.5 to 0.5
- user_basis: float32 [65536, 128], P('users'), may hold values from -6 to 6
- user_counts: int32 [128], P('users'), may hold values from 256 to 512, as said below
Outputs:
- basis: float32 [65536, 128], P('users')
- core_out: float32 [128, 512], replicated
The draws below stay inside these ranges and needn't reach their ends.
Inputs may be any that keep to these rules, and one draw needn't show every extreme that they name: `tile_owner`: among the 128 tiles of one device (aligned blocks of 128 rows), at most 2 name the same owner, and this is reached. `user_counts`: rows of a device at and beyond its count carry no events; some device has 512 live rows and some 512 // 2. tile_weights[t, :, u] is zero for u >= user_counts[t // 128].
All inputs are finite; a program needn't handle non-finite values.
Results may differ from the reference program's by a relative error of at most 0.006.
Values may be sent and summed in bfloat16 or wider, within the bound.
A program may use at most 128 MiB of HBM per device.

```python
import math
import jax
import jax.numpy as jnp
import numpy as np
from jax import lax

RU = 128
RI = 64
RC = 8
CTX = 512
CB = 8
IBLK = 128
U_DEV = 512
SLOTS = 2
TD = 128
IBD = 16
USERS = 65536
TILES = 16384
ITEM_BLOCKS = 2048
N_USERS = 128


def counts_common(key):
    base_key = jax.random.fold_in(key, 7301)
    first_key, second_key, third_key = jax.random.split(base_key, 3)
    counts = jax.random.randint(first_key, (N_USERS,), U_DEV // 2, U_DEV + 1)
    fullest = jax.random.randint(second_key, (), 0, N_USERS)
    counts = counts.at[fullest].set(U_DEV)
    emptiest = (fullest + 1 + jax.random.randint(third_key, (), 0, N_USERS - 1)) % N_USERS
    counts = counts.at[emptiest].set(U_DEV // 2)
    return counts.astype(jnp.int32)


def draw_user_counts(key, part):
    return counts_common(key)


def draw_tile_weights(key, part):
    counts = counts_common(key)
    value_key = jax.random.fold_in(key, 9157)
    values = jnp.clip(jax.random.normal(value_key, (TILES, IBLK, U_DEV), jnp.float32), -6.0, 6.0)
    owner_of = jnp.arange(TILES, dtype=jnp.int32) // TD
    limit = counts[owner_of]
    living = jnp.arange(U_DEV, dtype=jnp.int32)[None, :] < limit[:, None]
    values = jnp.where(living[:, None, :], values, jnp.zeros_like(values))
    return values.astype(jnp.bfloat16)


def plant(entries, rng, smallest, largest):
    dims = entries.shape
    index_at = [jax.random.randint(jax.random.fold_in(rng, axis), (), 0, dims[axis]) for axis in range(len(dims))]
    entries = entries.at[tuple(index_at)].set(smallest)
    longest = dims.index(max(dims))
    index_at[longest] = (index_at[longest] + 1) % dims[longest]
    return entries.at[tuple(index_at)].set(largest)


def block_scale(key, extent, cuts, smallest, high):
    gain, own = 1.0, jax.random.fold_in(key, 6)
    for position, shards_of in cuts:
        steps = jnp.exp(jax.random.uniform(jax.random.fold_in(own, position), (shards_of,), jnp.float32, smallest / len(cuts), high / len(cuts)))
        gain = gain * jnp.repeat(steps, extent[position] // shards_of).reshape([-1 if axis == position else 1 for axis in range(len(extent))])
    return gain


def assign_block(own_key, own, number, rows, count, top, most, slope):
    order = jax.random.permutation(own_key, count)
    packed, ordinary = shares(count, rows * top, most, slope, True), shares(count, rows * top, most, slope, False)
    places = jnp.arange(count)

    def named(lengths, offset_by):
        used = int((lengths > 0).sum())
        fixed = max(1, used // 4)
        shifted = fixed + (places - fixed + offset_by * (used - fixed)) % max(1, count - fixed)
        return jnp.zeros((count,), jnp.int32).at[order[jnp.where(places < fixed, places, shifted)]].set(jnp.asarray(lengths, jnp.int32))

    lengths = jnp.where(number % 4 == 0, named(packed, number // 4), named(ordinary, number - number // 4 - 1))
    mixed = jax.random.permutation(jax.random.fold_in(own, 3), count)
    donor, taker = mixed[0:count // 2 * 2:2], mixed[1:count // 2 * 2:2]
    slack = jnp.minimum(lengths[donor] - 1, most - lengths[taker]) // 2
    slack = jnp.where((donor == order[0]) | (taker == order[0]) | (lengths[taker] == 0), 0, jnp.maximum(slack, 0))
    shifted = jax.random.randint(jax.random.fold_in(own, 4), (count // 2,), 0, 1 << 20) % (slack + 1)
    lengths = lengths.at[donor].add(-shifted).at[taker].add(shifted)
    labels = jnp.searchsorted(jnp.cumsum(lengths), jnp.arange(rows * top), side="right").astype(jnp.int32)
    table = labels.reshape(top, rows).T
    table = table[jax.random.permutation(jax.random.fold_in(own, 1), rows)]
    offset_by = jax.random.randint(jax.random.fold_in(own, 2), (rows, 1), 0, top)
    return jnp.take_along_axis(table, (jnp.arange(top)[None, :] + offset_by) % top, axis=1)


def shares(count, total, reach, skew, full):
    weights = [(1 << 20) // math.isqrt(grade ** skew) + 1 for grade in range(1, count + 1)]
    largest = reach if full else min(reach, max(-(-total // count), total * weights[0] // sum(weights)))
    least = 1 if total - largest >= count - 1 else 0
    given, surplus = [largest] + [least] * (count - 1), total - largest - least * (count - 1)
    while surplus > 0:
        candidates = [i for i in range(1, count) if given[i] < largest] or [i for i in range(1, count) if given[i] < reach]
        mass, left = sum([weights[i] for i in candidates]), surplus
        for i in candidates:
            extra = min(reach - given[i], max(1, left * weights[i] // mass), surplus)
            given[i] = given[i] + extra
            surplus = surplus - extra
    return np.array(given)


def scatter_about(own_key, dims, width, most, cuts=(), kind=jnp.bfloat16):
    loudness = block_scale(own_key, dims, cuts, -0.22, 0.18) if cuts else 1.0
    result = jax.random.normal(own_key, dims, jnp.float32) * width * loudness
    return jnp.minimum(jnp.maximum(result, -most), most).astype(kind)


def setup_inputs(seed: int = 0) -> dict:
    seeds = jax.random.split(jax.random.key(seed), 10)
    tile_owner_keys = jax.random.split(jax.random.fold_in(seeds[0], 1), TILES // TD)
    tile_owner_turns = jax.random.permutation(jax.random.fold_in(seeds[0], 3), TILES // TD)
    tile_owner = jax.vmap(lambda own, number: assign_block(jax.random.fold_in(seeds[0], 2), own, number, TD, N_USERS, 1, SLOTS, 2))(tile_owner_keys, tile_owner_turns).reshape((TILES, 1))
    tile_slot = plant(jax.random.randint(seeds[1], (TILES,), 0, IBD), jax.random.fold_in(seeds[1], 1), 0, IBD - 1).astype(jnp.int32)
    tile_cblock = plant(jax.random.randint(seeds[2], (TILES,), 0, CTX // CB), jax.random.fold_in(seeds[2], 1), 0, (CTX // CB) - 1).astype(jnp.int32)
    tile_context = plant(jax.random.randint(seeds[3], (TILES, U_DEV), 0, CB), jax.random.fold_in(seeds[3], 1), 0, CB - 1).astype(jnp.int32)
    tile_weights = draw_tile_weights(jax.random.fold_in(seeds[9], 71), 0)
    item_factors = scatter_about(seeds[5], (ITEM_BLOCKS, RI, IBLK), IBLK ** -0.5, 0.5, ((0, 128),))
    context_factors = scatter_about(seeds[6], (RC, CTX), TD ** -0.5, 0.5)
    user_basis = scatter_about(seeds[7], (USERS, RU), 1.0, 6.0, ((0, 128),), jnp.float32)
    user_counts = draw_user_counts(jax.random.fold_in(seeds[9], 71), 0)
    return dict(tile_owner=tile_owner, tile_slot=tile_slot, tile_cblock=tile_cblock, tile_context=tile_context, tile_weights=tile_weights, item_factors=item_factors, context_factors=context_factors, user_basis=user_basis, user_counts=user_counts)


def reference(tile_owner, tile_slot, tile_cblock, tile_context, tile_weights, item_factors, context_factors, user_basis, user_counts):
    lookup = context_factors.astype(jnp.float32)
    factors_all = item_factors

    def device_rows(device_pack):
        owners, slots_of, cblocks, contexts, weights, count = device_pack
        blocks = factors_all[owners * IBD + slots_of].astype(jnp.float32)
        products = jnp.einsum('tai,tiu->tau', blocks, weights.astype(jnp.float32)).astype(jnp.bfloat16)
        columns = cblocks[:, None] * CB + contexts
        context_values = lookup[:, columns]
        rows_out = jnp.einsum('rtu,tau->rau', context_values, products.astype(jnp.float32))
        rows_out = rows_out.reshape(RC * RI, U_DEV)
        living = jnp.arange(U_DEV) < count
        rows_out = jnp.where(living[None, :], rows_out, jnp.zeros_like(rows_out))
        return rows_out.T
    device_pack = (tile_owner[:, 0].reshape(N_USERS, TD), tile_slot.reshape(N_USERS, TD), tile_cblock.reshape(N_USERS, TD), tile_context.reshape(N_USERS, TD, U_DEV), tile_weights.reshape(N_USERS, TD, IBLK, U_DEV), user_counts)
    ydata = lax.map(device_rows, device_pack).reshape(USERS, RC * RI)
    projection = jnp.dot(ydata.T, user_basis, precision=lax.Precision.HIGHEST)
    projected = jnp.dot(ydata, projection, precision=lax.Precision.HIGHEST)
    factor_q, factor_r = jnp.linalg.qr(projected)
    sign_fix = jnp.sign(jnp.diagonal(factor_r))
    basis = factor_q * sign_fix[None, :] * jnp.sqrt(jnp.float32(USERS))
    core_out = jnp.dot(basis.T, ydata, precision=lax.Precision.HIGHEST) / jnp.float32(USERS)
    return (basis, core_out)
```

```python
import functools

import jax
import jax.numpy as jnp
from jax import lax
from jax.experimental import pallas as pl
from jax.experimental.pallas import tpu as pltpu
from jax.sharding import PartitionSpec as P

MESH = pl.DeviceIdType.MESH
F32, BF16 = jnp.float32, jnp.bfloat16
NN = (((1,), (0,)), ((), ()))
NT = (((1,), (1,)), ((), ()))
TN = (((0,), (0,)), ((), ()))
BLOCKS = [(i, j) for i in range(4) for j in range(i, 4)]
TILES = 224
HALF, QUART, SIXT = 112, 28, 7
PANEL = 16
CB = 8
SLOTS = 2


def split(x):
    high = x.astype(BF16)
    return high, (x - high.astype(F32)).astype(BF16)


def dot1(a, b, dims):
    return lax.dot_general(a, b, dims, preferred_element_type=F32)


def dot3(a, b, dims):
    ah, al = split(a)
    bh, bl = split(b)
    return dot1(ah, bh, dims) + (dot1(ah, bl, dims) + dot1(al, bh, dims))


def tail_kernel(users, yt_ref, u_ref, basis_ref, core_ref, yh, yl, part, halfr, half, r1, q, r2, s2, r3,
                full, sfull, pfull, aug, send_sem, recv_sem):
    me = lax.axis_index("users")
    core = me % 2
    x, z, y = (me // 2) % 4, (me // 8) % 4, me // 32
    pos1 = x * (1 - core) + y * core
    pos2 = y * (1 - core) + z * core
    pos3 = z * (1 - core) + x * core
    str1 = 2 * (1 - core) + 32 * core
    str2 = 32 * (1 - core) + 8 * core
    str3 = 8 * (1 - core) + 2 * core
    partner = me + 1 - 2 * core

    def peer(pos, stride, off):
        there = (pos + off) % 4
        return there, me + (there - pos) * stride

    barrier = pltpu.get_barrier_semaphore()
    pl.semaphore_signal(barrier, inc=1, device_id=(partner,), device_id_type=MESH)
    for pos, stride in ((pos1, str1), (pos2, str2), (pos3, str3)):
        for off in (1, 2, 3):
            pl.semaphore_signal(barrier, inc=1, device_id=(peer(pos, stride, off)[1],), device_id_type=MESH)

    yh[...], yl[...] = split(yt_ref[...])
    uh, ul = split(u_ref[...])
    b = 0
    for i in range(4):
        rows = pl.ds(i * 128, 128)
        right = pl.ds(i * 128, 512 - i * 128)
        ah, al = yh[rows, :], yl[rows, :]
        s = dot1(ah, yh[right, :], NT) + (dot1(ah, yl[right, :], NT) + dot1(al, yh[right, :], NT))
        for j in range(i, 4):
            k = j - i
            part[pl.ds(b * 16, 16)] = s[:, k * 128:(k + 1) * 128].reshape(16, 8, 128)
            b += 1
    for i in range(4):
        rows = pl.ds(i * 128, 128)
        ah, al = yh[rows, :], yl[rows, :]
        p = dot1(ah, uh, NN) + (dot1(ah, ul, NN) + dot1(al, uh, NN))
        part[pl.ds((10 + i) * 16, 16)] = p.reshape(16, 8, 128)

    pl.semaphore_wait(barrier, 10)

    def copy(src, dst, n, device):
        return pltpu.make_async_remote_copy(src_ref=src, dst_ref=dst, send_sem=send_sem.at[n],
                                            recv_sem=recv_sem.at[n], device_id=(device,), device_id_type=MESH)

    c = copy(part.at[pl.ds((1 - core) * HALF, HALF)], halfr, 0, partner)
    c.start()
    c.wait()
    half[...] = part[pl.ds(core * HALF, HALF)] + halfr[...]

    copies = []
    for off in (1, 2, 3):
        there, device = peer(pos1, str1, off)
        c = copy(half.at[pl.ds(there * QUART, QUART)], r1.at[off - 1], off, device)
        c.start()
        copies.append(c)
    for c in copies:
        c.wait()
    q[...] = (half[pl.ds(pos1 * QUART, QUART)] + r1[0]) + (r1[1] + r1[2])

    copies = []
    for off in (1, 2, 3):
        there, device = peer(pos2, str2, off)
        c = copy(q.at[pl.ds(there * SIXT, SIXT)], r2.at[off - 1], 3 + off, device)
        c.start()
        copies.append(c)
    for c in copies:
        c.wait()
    mine = (q[pl.ds(pos2 * SIXT, SIXT)] + r2[0]) + (r2[1] + r2[2])
    s2[...] = mine

    copies = []
    for off in (1, 2, 3):
        there, device = peer(pos3, str3, off)
        c = copy(s2, r3.at[pos3], 6 + off, device)
        c.start()
        copies.append(c)
    r3[pos3] = mine
    for c in copies:
        c.wait()
    at2 = core * HALF + pos1 * QUART + pos2 * SIXT
    full[pl.ds(at2, SIXT)] = (r3[0] + r3[1]) + (r3[2] + r3[3])

    copies = []
    for off in (1, 2, 3):
        there, device = peer(pos2, str2, off)
        c = copy(full.at[pl.ds(at2, SIXT)], full.at[pl.ds(at2, SIXT)], 9 + off, device)
        c.start()
        copies.append(c)
    for c in copies:
        c.wait()
    at1 = core * HALF + pos1 * QUART
    copies = []
    for off in (1, 2, 3):
        there, device = peer(pos1, str1, off)
        c = copy(full.at[pl.ds(at1, QUART)], full.at[pl.ds(at1, QUART)], 12 + off, device)
        c.start()
        copies.append(c)
    for c in copies:
        c.wait()
    c = copy(full.at[pl.ds(core * HALF, HALF)], full.at[pl.ds(core * HALF, HALF)], 16, partner)
    c.start()
    c.wait()

    for b, (i, j) in enumerate(BLOCKS):
        blk = full[pl.ds(b * 16, 16)].reshape(128, 128)
        sfull[pl.ds(i * 128, 128), pl.ds(j * 128, 128)] = blk
        if i < j:
            sfull[pl.ds(j * 128, 128), pl.ds(i * 128, 128)] = blk.T
    for i in range(4):
        pfull[pl.ds(i * 128, 128), :] = full[pl.ds((10 + i) * 16, 16)].reshape(128, 128)
    p = pfull[...]
    t = dot3(p.T, sfull[...], NN)
    g = dot3(t, p, NN)
    linv = cholesky_inverse(g, aug)
    scale = float(users) ** 0.5
    core_ref[...] = dot3(linv, t, NN) * (scale / users)
    m = dot3(p, linv, NT) * scale
    mh, ml = split(m)
    basis_ref[...] = dot1(yh[...], mh, TN) + (dot1(yh[...], ml, TN) + dot1(yl[...], mh, TN))


def cholesky_inverse(g, aug):
    n = g.shape[0]
    r0 = lax.broadcasted_iota(jnp.int32, (n, n), 0)
    c0 = lax.broadcasted_iota(jnp.int32, (n, n), 1)
    aug[:, pl.ds(0, n)] = g
    aug[:, pl.ds(n, n)] = (r0 == c0).astype(F32)
    sub = lax.broadcasted_iota(jnp.int32, (PANEL, n), 0)
    for k in range(0, n, PANEL):
        left = aug[pl.ds(k, PANEL), pl.ds(0, n)]
        right = aug[pl.ds(k, PANEL), pl.ds(n, n)]
        for j in range(PANEL):
            col = jnp.broadcast_to(left[:, k + j:k + j + 1], (PANEL, n))
            root = lax.rsqrt(col[j:j + 1, :])
            lrow = left[j:j + 1, :] * root
            rrow = right[j:j + 1, :] * root
            mult = jnp.where(sub > j, col * root, 0.0)
            left = jnp.where(sub == j, lrow, left - mult * lrow)
            right = jnp.where(sub == j, rrow, right - mult * rrow)
        aug[pl.ds(k, PANEL), pl.ds(n, n)] = right
        if k + PANEL < n:
            below = n - k - PANEL
            rest = pl.ds(k + PANEL, below)
            lh, ll = split(left)
            rh, rl = split(right)
            th, tl = lh[:, k + PANEL:], ll[:, k + PANEL:]
            aug[rest, pl.ds(0, n)] -= dot1(th, lh, TN) + (dot1(th, ll, TN) + dot1(tl, lh, TN))
            aug[rest, pl.ds(n, n)] -= dot1(th, rh, TN) + (dot1(th, rl, TN) + dot1(tl, rh, TN))
    return aug[:, pl.ds(n, n)]


def tail(yt, user_basis, users):
    vm = pl.BlockSpec(memory_space=pltpu.VMEM)
    return pl.pallas_call(
        functools.partial(tail_kernel, users),
        out_shape=(jax.ShapeDtypeStruct((512, 128), F32), jax.ShapeDtypeStruct((128, 512), F32)),
        in_specs=[vm, vm],
        out_specs=(vm, vm),
        scratch_shapes=[
            pltpu.VMEM((512, 512), BF16),
            pltpu.VMEM((512, 512), BF16),
            pltpu.VMEM((TILES, 8, 128), F32),
            pltpu.VMEM((HALF, 8, 128), F32),
            pltpu.VMEM((HALF, 8, 128), F32),
            pltpu.VMEM((3, QUART, 8, 128), F32),
            pltpu.VMEM((QUART, 8, 128), F32),
            pltpu.VMEM((3, SIXT, 8, 128), F32),
            pltpu.VMEM((SIXT, 8, 128), F32),
            pltpu.VMEM((4, SIXT, 8, 128), F32),
            pltpu.VMEM((TILES, 8, 128), F32),
            pltpu.VMEM((512, 512), F32),
            pltpu.VMEM((512, 128), F32),
            pltpu.VMEM((128, 256), F32),
            pltpu.SemaphoreType.DMA((17,)),
            pltpu.SemaphoreType.DMA((17,)),
        ],
        compiler_params=pltpu.CompilerParams(collective_id=0, has_side_effects=True),
        name="tail",
    )(yt, user_basis)


def body(
    tile_owner,
    tile_slot,
    tile_cblock,
    tile_context,
    tile_weights,
    item_factors,
    context_factors,
    user_basis,
    user_counts,
):
    devices = lax.axis_size("users")
    owners = tile_owner[:, 0]
    rank_c = context_factors.shape[0]
    rank_i = item_factors.shape[1]
    block_len = item_factors.shape[2]
    user_rows = tile_weights.shape[2]
    total_users = user_rows * devices
    ctx_block = tile_context.shape[0] * 0 + CB
    owner_hits = owners[:, None] == jnp.arange(devices, dtype=jnp.int32)[None, :]
    owner_ints = owner_hits.astype(jnp.int32)
    earlier = jnp.cumsum(owner_ints, axis=0) - owner_ints
    position = jnp.sum(earlier * owner_ints, axis=1)
    placed = owner_hits[:, :, None] & (
        position[:, None, None] == jnp.arange(SLOTS, dtype=jnp.int32)[None, None, :]
    )
    requests = jnp.sum(jnp.where(placed, tile_slot[:, None, None], 0), axis=0)
    found = item_factors[lax.all_to_all(requests, "users", split_axis=0, concat_axis=0, tiled=True)]
    fetched = lax.all_to_all(found, "users", split_axis=0, concat_axis=0, tiled=True)
    blocks = fetched.reshape(devices * SLOTS, rank_i, block_len)[owners * SLOTS + position]
    products = jnp.einsum(
        "tai,tiu->tau", blocks, tile_weights, preferred_element_type=jnp.float32
    ).astype(jnp.bfloat16)
    lookup = context_factors.astype(jnp.float32).reshape(rank_c, -1, ctx_block)
    chosen = (tile_cblock[:, None] == jnp.arange(lookup.shape[1], dtype=jnp.int32)[None, :]).astype(
        jnp.float32
    )
    block_values = jnp.einsum("rbk,tb->trk", lookup, chosen).astype(jnp.bfloat16)
    context_hits = (
        tile_context[:, None, :] == jnp.arange(ctx_block, dtype=jnp.int32)[None, :, None]
    ).astype(jnp.bfloat16)
    context_values = jnp.einsum(
        "trk,tku->tru", block_values, context_hits, preferred_element_type=jnp.float32
    ).astype(jnp.bfloat16)
    ytrans = jnp.einsum(
        "tru,tau->rau", context_values, products, preferred_element_type=jnp.float32
    )
    ytrans = ytrans.reshape(rank_c * rank_i, user_rows)
    living = jnp.arange(user_rows, dtype=jnp.int32) < user_counts[0]
    ytrans = jnp.where(living[None, :], ytrans, jnp.zeros_like(ytrans))
    basis, core_out = tail(ytrans, user_basis, total_users)
    return (basis, core_out)


def solution(mesh):
    return jax.shard_map(
        body,
        mesh=mesh,
        in_specs=(
            P("users", None),
            P("users"),
            P("users"),
            P("users", None),
            P("users", None, None),
            P("users", None, None),
            P(),
            P("users", None),
            P("users"),
        ),
        out_specs=(P("users", None), P()),
        check_vma=False,
    )
```
